32 devices in a mesh: grp: 2 (over y), pair: 4 (over z), rep: 2 (over x), sub: 2 (over core).
Axes of the slice: x: 2, y: 2, z: 4, core: 2. Of those that a mesh axis runs over, the one named last changes fastest.
Arguments:
- cholesky: bfloat16 [256, 640, 640], P('sub', 'pair'), may hold values from -0.015625 to 0.015625
- trial_orbitals: bfloat16 [640, 192], replicated, may hold values from -0.25 to 0.25
- walkers: bfloat16 [32, 640, 192], P(('grp', 'pair', 'rep'), None, 'sub'), parts along dimension 0, may hold values from -6 to 6
- intersection_inverse: bfloat16 [32, 192, 192], P(('grp', 'pair', 'rep')), parts along dimension 0, may hold values from -0.4375 to 0.4375
- noise_stream: float32 [2048], P('grp'), parts along dimension 0, may hold values from -6 to 6
- offsets: int32 [32], P('grp'), parts along dimension 0, may hold values from 0 to 768
- parents: int32 [32], P(('grp', 'pair', 'rep')), parts along dimension 0, may hold values from 0 to 7
Outputs:
- new_walkers: bfloat16 [32, 640, 192], P(('grp', 'pair', 'rep'), None, 'sub'), parts along dimension 0
- force_bias: float32 [32, 256], P(('grp', 'pair', 'rep'), 'sub'), parts along dimension 0
The draws below stay inside these ranges and needn't reach their ends.
There are 2 independent parts, one for each index of `grp`. The reference program is written for one: setup_inputs(seed, part) draws one part's arguments, and reference() takes and returns one part's arrays. A program takes and returns all parts, laid end to end along the dimension named above; an argument that names none is the same for every part. Nothing has to cross between parts.
All inputs are finite; a program needn't handle non-finite values.
Results may differ from the reference program's by a relative error of at most 0.035.
Values may be sent and summed in bfloat16 or wider, within the bound.
No kernel may reach another device: no remote copies, remote signals or barrier semaphores. Data moves between devices by JAX's collectives and lax.ppermute only.
A program may use at most 64 MiB of HBM per device.

```python
import math
import jax
import jax.numpy as jnp
import numpy as np

M = 640
NEL = 192
NCHOL = 256
TAYLOR = 6
WALK_DEV = 2
W = 16
NSTREAM = 1024
N_PAIR = 4
N_REP = 2


def with_ends(drawn, stream_key, low, top_value):
    dims = drawn.shape
    spot = [jax.random.randint(jax.random.fold_in(stream_key, axis), (), 0, dims[axis]) for axis in range(len(dims))]
    drawn = drawn.at[tuple(spot)].set(low)
    longest = dims.index(max(dims))
    spot[longest] = (spot[longest] + 1) % dims[longest]
    return drawn.at[tuple(spot)].set(top_value)


def shard_levels(own_key, dims, split, least, high):
    loudness, own = 1.0, jax.random.fold_in(own_key, 6)
    for position, shards_of in split:
        draws = jnp.exp(jax.random.uniform(jax.random.fold_in(own, position), (shards_of,), jnp.float32, least / len(split), high / len(split)))
        loudness = loudness * jnp.repeat(draws, dims[position] // shards_of).reshape([-1 if axis == position else 1 for axis in range(len(dims))])
    return loudness


def cumulative_ranks(count, lean):
    loads = [(1 << 20) // math.isqrt(standing ** lean) + 1 for standing in range(1, count + 1)]
    deviation = 1 + sum(loads) // (1 << 30)
    return np.cumsum(np.array([max(1, weight // deviation) for weight in loads]))


def ranked(stream_key, shape, number_of, slope):
    grid = cumulative_ranks(number_of, slope)
    lot = jax.random.randint(jax.random.fold_in(stream_key, 1), shape, 0, int(grid[number_of - 1]))
    standing = jnp.searchsorted(jnp.asarray(grid, jnp.int32), lot, side="right")
    return jax.random.permutation(jax.random.fold_in(stream_key, 2), number_of)[standing].astype(jnp.int32)


def gaussian(rng, dims, width, limit, shards=(), kind=jnp.bfloat16):
    array = width * jax.random.normal(rng, dims, jnp.float32)
    if shards:
        array = array * shard_levels(rng, dims, shards, -0.22, 0.18)
    return jnp.clip(array, -limit, limit).astype(kind)


def setup_inputs(seed: int = 0, part: int = 0) -> dict:
    key_of = jax.random.split(jax.random.key(seed), 8)
    part_splits = jax.random.split(jax.random.fold_in(key_of[7], part), 8)
    return {
        "cholesky": gaussian(key_of[0], (NCHOL, M, M), (M * NEL) ** -0.5, 0.015625, ((0, 2), (1, 4))),
        "trial_orbitals": gaussian(key_of[1], (M, NEL), M ** -0.5, 0.25),
        "walkers": gaussian(part_splits[2], (W, M, NEL), 1.0, 6.0, ((0, 8), (2, 2))),
        "intersection_inverse": gaussian(part_splits[3], (W, NEL, NEL), NEL ** -0.5, 0.4375, ((0, 8),)),
        "noise_stream": gaussian(part_splits[4], (NSTREAM,), 1.0, 6.0, (), jnp.float32),
        "offsets": with_ends(jax.random.randint(part_splits[5], (W,), 0, NSTREAM - NCHOL + 1), jax.random.fold_in(part_splits[5], 1), 0, NSTREAM - NCHOL).astype(jnp.int32),
        "parents": with_ends(ranked(part_splits[6], (W,), N_PAIR * WALK_DEV, 2), jax.random.fold_in(part_splits[6], 3), 0, (N_PAIR * WALK_DEV) - 1).astype(jnp.int32),
    }


field_scale = 1.6


def reference(cholesky, trial_orbitals, walkers, intersection_inverse, noise_stream, offsets, parents):
    chol_wide = cholesky.astype(jnp.float32)
    half_rotated = jnp.einsum('gpq,qi->gpi', chol_wide, trial_orbitals.astype(jnp.float32)).astype(jnp.bfloat16)
    mixed = jnp.einsum('wpj,wji->wpi', walkers.astype(jnp.float32), intersection_inverse.astype(jnp.float32)).astype(jnp.bfloat16)
    force_bias = jnp.einsum('wpi,gpi->wg', mixed.astype(jnp.float32), half_rotated.astype(jnp.float32))
    window_index = offsets[:, None] + jnp.arange(NCHOL, dtype=jnp.int32)[None, :]
    fields = (noise_stream[window_index] - force_bias).astype(jnp.bfloat16)
    potential = (field_scale * jnp.einsum('wg,gpq->wpq', fields.astype(jnp.float32), chol_wide)).astype(jnp.bfloat16)
    potential_wide = potential.astype(jnp.float32)
    taylor_term = walkers
    summed = walkers.astype(jnp.float32)
    for degree in range(1, TAYLOR + 1):
        product = jnp.einsum('wpq,wqi->wpi', potential_wide, taylor_term.astype(jnp.float32))
        taylor_term = (product / jnp.float32(degree)).astype(jnp.bfloat16)
        summed = summed + taylor_term.astype(jnp.float32)
    propagated = summed.astype(jnp.bfloat16)
    row_walkers = propagated.reshape(N_PAIR, N_REP, WALK_DEV, M, NEL)
    row_walkers = jnp.transpose(row_walkers, (1, 0, 2, 3, 4)).reshape(N_REP, N_PAIR * WALK_DEV, M, NEL)
    parent_grid = parents.reshape(N_PAIR, N_REP, WALK_DEV)
    row_numbers = jnp.arange(N_REP, dtype=jnp.int32)[None, :, None]
    new_walkers = row_walkers[row_numbers, parent_grid].reshape(W, M, NEL)
    return new_walkers, force_bias
```

```python
import functools

import jax
import jax.numpy as jnp
from jax import lax
from jax.experimental import pallas as pl
from jax.experimental.pallas import tpu as pltpu
from jax.sharding import PartitionSpec as P

TAYLOR = 6


field_scale = 1.6

LANES = 128
STEP = 16


def general_shards(cholesky, trial_orbitals, walkers, intersection_inverse, noise_stream, offsets, parents):
    chol_count = cholesky.shape[0]
    walk_count = walkers.shape[0]
    pair_size = lax.axis_size("pair")
    rep_size = lax.axis_size("rep")
    pair_index = lax.axis_index("pair")
    rep_index = lax.axis_index("rep")
    sub_index = lax.axis_index("sub")
    half_rotated = jnp.einsum(
        "gpq,qi->gpi", cholesky, trial_orbitals, preferred_element_type=jnp.float32
    ).astype(jnp.bfloat16)
    whole_walkers = lax.all_gather(walkers, "sub", axis=2, tiled=True)
    mixed = jnp.einsum(
        "wpj,wji->wpi", whole_walkers, intersection_inverse, preferred_element_type=jnp.float32
    ).astype(jnp.bfloat16)
    mixed_rows = lax.all_to_all(mixed, "pair", split_axis=1, concat_axis=0, tiled=True)
    partial_bias = jnp.einsum(
        "jpi,gpi->jg", mixed_rows, half_rotated, preferred_element_type=jnp.float32
    )
    window_start = sub_index * chol_count
    vector_steps = jnp.arange(chol_count, dtype=jnp.int32)

    def window_fields(offset_value, bias_row):
        drawn = noise_stream[offset_value + window_start + vector_steps]
        return (drawn - bias_row).astype(jnp.bfloat16)

    offsets_grid = offsets.reshape(pair_size, rep_size, walk_count)
    bias_totals = lax.psum(partial_bias.astype(jnp.bfloat16), "pair").astype(jnp.float32)
    row_offsets = lax.dynamic_index_in_dim(offsets_grid, rep_index, 1, False).reshape(-1)
    fields = jax.vmap(window_fields)(row_offsets, bias_totals)
    force_bias = lax.dynamic_slice_in_dim(bias_totals, pair_index * walk_count, walk_count, 0)
    partial_potential = jnp.einsum(
        "jg,gpq->jpq", fields, cholesky, preferred_element_type=jnp.float32
    )
    summed_potential = lax.psum(partial_potential.astype(jnp.bfloat16), "sub").astype(jnp.float32)
    potential = lax.all_to_all(
        (field_scale * summed_potential).astype(jnp.bfloat16),
        "pair",
        split_axis=0,
        concat_axis=1,
        tiled=True,
    )
    taylor_term = walkers
    summed = walkers.astype(jnp.float32)
    for degree in range(1, TAYLOR + 1):
        product = jnp.einsum(
            "wpq,wqi->wpi", potential, taylor_term, preferred_element_type=jnp.float32
        )
        taylor_term = (product / jnp.float32(degree)).astype(jnp.bfloat16)
        summed = summed + taylor_term.astype(jnp.float32)
    propagated = summed.astype(jnp.bfloat16)
    portion = lax.all_gather(propagated, "pair", axis=0, tiled=True)
    row_count = portion.shape[0]
    positions = jnp.arange(row_count, dtype=jnp.int32)
    selector = (parents[:, None] == positions[None, :]).astype(jnp.bfloat16)
    chosen = jnp.einsum("kr,rpi->kpi", selector, portion, preferred_element_type=jnp.float32)
    new_walkers = chosen.astype(jnp.bfloat16)
    return (new_walkers, force_bias)


VMEM = pl.BlockSpec(memory_space=pltpu.VMEM)
SMEM = pl.BlockSpec(memory_space=pltpu.SMEM)
HBM = pl.BlockSpec(memory_space=pltpu.HBM)
f32 = jnp.float32
bf16 = jnp.bfloat16


def call(body, outs, in_specs, limit, flops, scratch=(), out_specs=None):
    return pl.pallas_call(
        body,
        out_shape=outs,
        in_specs=in_specs,
        out_specs=out_specs if out_specs is not None else jax.tree.map(lambda _: VMEM, outs),
        scratch_shapes=scratch,
        compiler_params=pltpu.CompilerParams(vmem_limit_bytes=limit),
        cost_estimate=pl.CostEstimate(flops=flops, bytes_accessed=1 << 16, transcendentals=0),
        name=body.func.__name__ if isinstance(body, functools.partial) else body.__name__,
    )


def mix_kernel(n_pair, own_ref, other_ref, inverse_ref, *refs):
    outs, whole = refs[:n_pair], refs[n_pair]
    b, s = lax.axis_index("pair"), lax.axis_index("sub")
    mine, theirs = own_ref[s], other_ref[s]
    low = jnp.where(s == 0, mine, theirs)
    high = jnp.where(s == 0, theirs, mine)
    turned = jnp.concatenate([low, high], axis=0).astype(f32)
    plain = turned.T.astype(bf16)
    mixed = jnp.dot(plain, inverse_ref[s], preferred_element_type=f32).astype(bf16)
    whole[...] = jnp.concatenate([mixed, plain], axis=1)
    rows = outs[0].shape[0]
    for x in range(n_pair):
        outs[x][...] = whole[pl.ds(pl.multiple_of((b ^ x) * rows, STEP), rows), :]


def rotate_kernel(n_pair, n_walk, chunk, chol_ref, trial_ref, noise_ref, offsets_ref, chol_out, half_out, spread_out, noise_out, sems):
    n_tile, n_chol, rows, _ = chol_out.shape
    copies = n_chol // chunk

    def copy(c, j):
        span = pl.ds(c * chunk, chunk)
        return pltpu.make_async_copy(
            chol_ref.at[span, :, pl.ds(j * LANES, LANES)], chol_out.at[j, span], sems.at[c, j]
        )

    for c in range(copies):
        for j in range(n_tile):
            copy(c, j).start()
    b, r, s = lax.axis_index("pair"), lax.axis_index("rep"), lax.axis_index("sub")
    n_rep = lax.axis_size("rep")
    for y in range(n_pair):
        for c in range(n_walk):
            walker = ((b ^ y) * n_rep + r) * n_walk + (s ^ c)
            start = offsets_ref[walker] + s * n_chol
            line = start // LANES
            shift = start - line * LANES
            last = noise_ref.shape[0] - 1
            pair = jnp.concatenate(
                [noise_ref[pl.ds(line, 1), :], noise_ref[pl.ds(jnp.minimum(line + 1, last), 1), :]], axis=1
            )
            moved = pltpu.roll(jnp.broadcast_to(pair, (8, 2 * LANES)), 2 * LANES - shift, 1)
            noise_out[pl.ds(y * n_walk + c, 1), :] = moved[:1, :LANES]
    row = lax.broadcasted_iota(jnp.int32, spread_out.shape, 0)
    lane = lax.broadcasted_iota(jnp.int32, spread_out.shape, 1)
    spread_out[...] = jnp.where(lane // STEP == row, 1.0, 0.0).astype(bf16)
    n_half, width = half_out.shape[0], trial_ref.shape[0]
    trial = trial_ref[...]

    def body(c, carry):
        for j in range(n_tile):
            copy(c, j).wait()
        span = pl.ds(c * chunk, chunk)
        block = jnp.concatenate([chol_out[j, span].reshape(chunk * rows, LANES) for j in range(n_tile)], axis=1)
        rotated = lax.dot_general(block, trial, (((1,), (1,)), ((), ())), preferred_element_type=f32).astype(bf16)
        if width < n_half * LANES:
            rotated = jnp.concatenate([rotated, jnp.zeros((chunk * rows, n_half * LANES - width), bf16)], axis=1)
        for h in range(n_half):
            half_out[h, span] = rotated[:, h * LANES : (h + 1) * LANES].reshape(chunk, rows, LANES)
        return carry

    lax.fori_loop(0, copies, body, 0)


def bias_kernel(n_el, own_ref, other_ref, half_ref, spread_ref, parents_ref, out_ref, left, lines):
    n_pair, rows, _ = own_ref.shape
    n_half, n_chol = half_ref.shape[0], half_ref.shape[1]
    width = n_half * LANES
    n_slot = 2 * n_pair
    blocks = rows // STEP
    for p in range(blocks):
        span = slice(p * STEP, (p + 1) * STEP)
        parts = [ref[y, span, :n_el] for y in range(n_pair) for ref in (own_ref, other_ref)]
        block = jnp.concatenate(parts, axis=0)
        if n_el < width:
            block = jnp.concatenate([block, jnp.zeros((n_slot * STEP, width - n_el), bf16)], axis=1)
        left[:, p * width : (p + 1) * width] = block
    many = 2 * LANES // STEP
    row = lax.broadcasted_iota(jnp.int32, (n_slot * STEP, 2 * LANES), 0)
    lane = lax.broadcasted_iota(jnp.int32, (n_slot * STEP, 2 * LANES), 1)
    same = row % STEP == lane % STEP

    def body(c, carry):
        span = pl.ds(c * many, many)
        total = jnp.zeros((n_slot * STEP, 2 * LANES), f32)
        for p in range(blocks):
            right = jnp.concatenate(
                [half_ref[h, span, p * STEP : (p + 1) * STEP, :].reshape(many * STEP, LANES) for h in range(n_half)], axis=1
            )
            total = total + lax.dot_general(
                left[:, p * width : (p + 1) * width], right, (((1,), (1,)), ((), ())), preferred_element_type=f32
            )
        kept = jnp.where(same, total, 0.0).reshape(n_slot, STEP, 2 * LANES).sum(axis=1)
        lines[:, pl.ds(pl.multiple_of(c * 2 * LANES, 2 * LANES), 2 * LANES)] = kept
        return carry

    lax.fori_loop(0, n_chol // many, body, 0)
    rest = lines[...]
    bias = jnp.zeros((n_slot, n_chol), f32)
    for _ in range(3):
        piece = rest.astype(bf16)
        bias = bias + lax.dot_general(piece, spread_ref[...], (((1,), (1,)), ((), ())), preferred_element_type=f32)
        rest = rest - piece.astype(f32)
    out_ref[:n_slot, :] = bias
    which = lax.broadcasted_iota(jnp.int32, (8, n_chol), 0)
    out_ref[n_slot:, :] = jnp.where(which == 0, parents_ref[0], parents_ref[1]).astype(f32)


def fields_kernel(n_pair, noise_ref, *refs):
    biases, bias_out, fields_out, picks_out = refs[:n_pair], *refs[n_pair:]
    b, s = lax.axis_index("pair"), lax.axis_index("sub")
    n_slot = 2 * n_pair
    total = biases[0][:n_slot, :]
    for x in range(1, n_pair):
        total = total + jnp.concatenate([biases[x][2 * (y ^ x) : 2 * (y ^ x) + 2, :] for y in range(n_pair)], axis=0)
    bias_out[pl.ds(s, 1), :] = total[:1]
    bias_out[pl.ds(1 - s, 1), :] = total[1:2]
    walker_fields = (noise_ref[...] - total).astype(bf16).astype(f32)
    ancestry = jnp.concatenate(
        [biases[y][pl.ds(n_slot + (s ^ c), 1), :] for y in range(n_pair) for c in range(2)], axis=0
    )
    chosen = jnp.zeros_like(total)
    for y in range(n_pair):
        for c in range(2):
            name = ((b ^ y) * 2 + (s ^ c)).astype(f32)
            chosen = chosen + jnp.where(ancestry == name, walker_fields[2 * y + c : 2 * y + c + 1], 0.0)
    fields_out[...] = chosen
    slot_name = lax.broadcasted_iota(jnp.int32, ancestry.shape, 1)
    mapped = ((slot_name // 2) ^ b) * 2 + ((slot_name % 2) ^ s)
    picks_out[...] = jnp.where(ancestry == mapped.astype(f32), 1.0, 0.0)


def potential_kernel(first, count, fields_ref, chol_ref, spread_ref, own_ref, send_ref, left):
    n_tile, n_chol, rows, _ = chol_ref.shape
    blocks = rows // STEP
    width = n_chol * STEP
    grown = jnp.dot(fields_ref[...].astype(bf16), spread_ref[...], preferred_element_type=f32)
    row = lax.broadcasted_iota(jnp.int32, (STEP, width), 0)
    lane = lax.broadcasted_iota(jnp.int32, (STEP, width), 1)
    same = row == lane % STEP
    for c in range(2):
        for k in range(count):
            slot = 2 * (first + k) + c
            at = (c * count + k) * STEP
            left[at : at + STEP, :] = jnp.where(same, jnp.broadcast_to(grown[slot : slot + 1], (STEP, width)), 0.0).astype(bf16)

    def body(i, carry):
        j = i // (blocks // 2)
        p = (i - j * (blocks // 2)) * 2
        spans = [pl.ds(pl.multiple_of((p + d) * STEP, STEP), STEP) for d in range(2)]
        right = jnp.concatenate([chol_ref[j, :, span, :].reshape(width, LANES) for span in spans], axis=1)
        product = jnp.dot(left[...], right, preferred_element_type=f32)
        for k in range(count):
            for d in range(2):
                lanes = slice(d * LANES, (d + 1) * LANES)
                own_ref[k, j, spans[d], :] = product[k * STEP : (k + 1) * STEP, lanes]
                at = (count + k) * STEP
                send_ref[k, j, spans[d], :] = product[at : at + STEP, lanes].astype(bf16)
        return carry

    lax.fori_loop(0, n_tile * (blocks // 2), body, 0)


def join_kernel(first, n_el, own_ref, other_ref, picks_ref, mine_ref, theirs_ref, *outs):
    n_pair = mine_ref.shape[0]
    n_tile = own_ref.shape[1]
    for k, out in enumerate(outs):
        out[:n_tile] = (field_scale * (own_ref[k] + other_ref[k].astype(f32))).astype(bf16)
        picked = jnp.zeros(mine_ref.shape[1:2] + (n_el,), f32)
        for y in range(n_pair):
            for c, ref in enumerate((mine_ref, theirs_ref)):
                slot = 2 * y + c
                weight = picks_ref[2 * (first + k) : 2 * (first + k) + 1, slot : slot + 1]
                picked = picked + weight * ref[y, :, n_el : 2 * n_el].astype(f32)
        picked = picked.astype(bf16)
        for h in range(out.shape[0] - n_tile):
            width = min(LANES, n_el - h * LANES)
            out[n_tile + h, :, :width] = picked[:, h * LANES : h * LANES + width]


def taylor_kernel(n_pair, n_tile, n_el, *refs):
    blocks, keep_ref, send_ref, term, total = refs[:n_pair], *refs[n_pair:]
    b, s = lax.axis_index("pair"), lax.axis_index("sub")
    rows = blocks[0].shape[1]

    def place(x):
        return pl.ds(pl.multiple_of((b ^ x) * rows, STEP), rows)

    n_half = blocks[0].shape[0] - n_tile
    for x in range(n_pair):
        start = jnp.concatenate(
            [blocks[x][n_tile + h, :, : min(LANES, n_el - h * LANES)] for h in range(n_half)], axis=1
        )
        term[place(x), :] = start
        total[x * rows : (x + 1) * rows, :] = start.astype(f32)
    matrix = jnp.concatenate(
        [jnp.concatenate([blocks[x][j] for j in range(n_tile)], axis=1) for x in range(n_pair)], axis=0
    )
    for degree in range(1, TAYLOR + 1):
        product = jnp.dot(matrix, term[...], preferred_element_type=f32)
        new = (product * f32(1.0 / degree)).astype(bf16)
        total[...] += new.astype(f32)
        if degree < TAYLOR:
            for x in range(n_pair):
                term[place(x), :] = new[x * rows : (x + 1) * rows]
    for x in range(n_pair):
        term[place(x), :] = total[x * rows : (x + 1) * rows, :].astype(bf16)
    turned = term[...].astype(f32).T.astype(bf16)
    half = n_el // 2
    low, high = turned[:half], turned[half:]
    keep_ref[...] = jnp.where(s == 0, low, high)
    send_ref[...] = jnp.where(s == 0, high, low)


def finish_kernel(keep_ref, other_ref, out_ref):
    s = lax.axis_index("sub")
    out_ref[s] = keep_ref[...]
    out_ref[1 - s] = other_ref[...]


def fast_shards(cholesky, trial_orbitals, walkers, intersection_inverse, noise_stream, offsets, parents):
    n_chol, rows, n_orb = cholesky.shape
    n_el = trial_orbitals.shape[1]
    n_walk, _, half_el = walkers.shape
    n_pair = lax.axis_size("pair")
    n_tile = n_orb // LANES
    n_half = pl.cdiv(n_el, LANES)
    n_slot = n_pair * n_walk
    chunk = 8

    def across(value, x):
        return lax.ppermute(value, "pair", [(i, i ^ x) for i in range(n_pair)])

    def swap(value):
        return lax.ppermute(value, "sub", [(0, 1), (1, 0)])

    turned = jnp.swapaxes(walkers, 1, 2)
    rows_out = call(
        functools.partial(mix_kernel, n_pair),
        [jax.ShapeDtypeStruct((rows, 2 * n_el), bf16)] * n_pair,
        [VMEM] * 3,
        8 << 20,
        2 * n_orb * n_el * n_el,
        [pltpu.VMEM((n_orb, 2 * n_el), bf16)],
    )(turned, swap(turned), intersection_inverse)
    arrived = [rows_out[0]] + [across(rows_out[x], x) for x in range(1, n_pair)]
    resident, half_rotated, spread, noise = call(
        functools.partial(rotate_kernel, n_pair, n_walk, chunk),
        [
            pltpu.VMEM((n_tile, n_chol, rows, LANES), bf16),
            pltpu.VMEM((n_half, n_chol, rows, LANES), bf16),
            pltpu.VMEM((n_chol, n_chol * STEP), bf16),
            pltpu.VMEM((n_slot, n_chol), f32),
        ],
        [HBM, VMEM, VMEM, SMEM],
        8 << 20,
        2 * n_chol * rows * n_orb * n_el,
        [pltpu.SemaphoreType.DMA((n_chol // chunk, n_tile))],
    )(cholesky, trial_orbitals.T, noise_stream.reshape(-1, LANES), offsets)
    mine = jnp.stack(arrived)
    theirs = swap(mine)
    partial_bias = call(
        functools.partial(bias_kernel, n_el),
        jax.ShapeDtypeStruct((n_slot + 8, n_chol), f32),
        [VMEM] * 4 + [SMEM],
        8 << 20,
        2 * n_slot * STEP * n_chol * rows * n_el,
        [
            pltpu.VMEM((n_slot * STEP, rows // STEP * n_half * LANES), bf16),
            pltpu.VMEM((n_slot, n_chol * STEP), f32),
        ],
    )(mine, theirs, half_rotated, spread, parents)
    biases = [partial_bias] + [across(partial_bias, x) for x in range(1, n_pair)]
    force_bias, fields, picks = call(
        functools.partial(fields_kernel, n_pair),
        [
            jax.ShapeDtypeStruct((n_walk, n_chol), f32),
            jax.ShapeDtypeStruct((n_slot, n_chol), f32),
            jax.ShapeDtypeStruct((n_slot, n_chol), f32),
        ],
        [VMEM] * (1 + n_pair),
        4 << 20,
        1 << 10,
    )(noise, *biases)
    got = [None] * n_pair
    half = n_pair // 2
    for first in (half, 0):
        own, send = call(
            functools.partial(potential_kernel, first, half),
            [
                jax.ShapeDtypeStruct((half, n_tile, rows, LANES), f32),
                jax.ShapeDtypeStruct((half, n_tile, rows, LANES), bf16),
            ],
            [VMEM] * 3,
            8 << 20,
            2 * n_pair * STEP * n_chol * rows * n_orb,
            [pltpu.VMEM((n_pair * STEP, n_chol * STEP), bf16)],
        )(fields, resident, spread)
        joined = call(
            functools.partial(join_kernel, first, n_el),
            [jax.ShapeDtypeStruct((n_tile + n_half, rows, LANES), bf16)] * half,
            [VMEM] * 5,
            8 << 20,
            1 << 10,
        )(own, swap(send), picks, mine, theirs)
        for k in range(half):
            x = first + k
            got[x] = across(joined[k], x) if x else joined[k]
    keep, give = call(
        functools.partial(taylor_kernel, n_pair, n_tile, n_el),
        [jax.ShapeDtypeStruct((half_el, n_orb), bf16)] * 2,
        [VMEM] * n_pair,
        16 << 20,
        2 * TAYLOR * n_orb * n_orb * n_el,
        [pltpu.VMEM((n_orb, n_el), bf16), pltpu.VMEM((n_orb, n_el), f32)],
    )(*got)
    new_turned = call(
        finish_kernel,
        jax.ShapeDtypeStruct((n_walk, half_el, n_orb), bf16),
        [VMEM] * 2,
        4 << 20,
        1 << 10,
    )(keep, swap(give))
    return (jnp.swapaxes(new_turned, 1, 2), force_bias)


def fits(mesh, cholesky, trial_orbitals, walkers, noise_stream):
    sizes = mesh.shape
    n_pair, n_sub = sizes["pair"], sizes["sub"]
    rows = cholesky.shape[1] // n_pair
    n_chol = cholesky.shape[0] // n_sub
    n_walk = walkers.shape[0] // (sizes["grp"] * n_pair * sizes["rep"])
    resident = n_chol * rows * (cholesky.shape[2] + 2 * LANES) * 2
    return (
        n_sub == 2
        and n_walk == 2
        and n_pair in (2, 4)
        and rows % (2 * STEP) == 0
        and cholesky.shape[2] % LANES == 0
        and n_chol == LANES
        and trial_orbitals.shape[1] <= 2 * LANES
        and noise_stream.shape[0] // sizes["grp"] % LANES == 0
        and resident <= 40 << 20
    )


def solution(mesh):
    in_specs = (
        P("sub", "pair", None),
        P(),
        P(("grp", "pair", "rep"), None, "sub"),
        P(("grp", "pair", "rep"), None, None),
        P("grp"),
        P("grp"),
        P(("grp", "pair", "rep")),
    )
    out_specs = (P(("grp", "pair", "rep"), None, "sub"), P(("grp", "pair", "rep"), "sub"))

    def step(cholesky, trial_orbitals, walkers, intersection_inverse, noise_stream, offsets, parents):
        body = fast_shards if fits(mesh, cholesky, trial_orbitals, walkers, noise_stream) else general_shards
        return jax.shard_map(body, mesh=mesh, in_specs=in_specs, out_specs=out_specs, check_vma=False)(
            cholesky, trial_orbitals, walkers, intersection_inverse, noise_stream, offsets, parents
        )

    return step
```
